32 devices in a mesh: seq: 16 (over z, y, x), dp: 2 (over core).
Axes of the slice: x: 2, y: 2, z: 4, core: 2. Of those that a mesh axis runs over, the one named last changes fastest.
Arguments:
- query_rows: bfloat16 [2, 2048, 1024], P('dp', 'seq'), may hold values from -6 to 6
- key_rows: bfloat16 [2, 2048, 1024], P('dp', 'seq'), may hold values from -6 to 6
- value_rows: bfloat16 [2, 2048, 1024], P('dp', 'seq'), may hold values from -6 to 6
- out_grad: bfloat16 [2, 2048, 1024], P('dp', 'seq'), may hold values from -6 to 6
- query_gain: float32 [1024], replicated, may hold values from 0.1 to 1.9
- key_gain: float32 [1024], replicated, may hold values from 0.1 to 1.9
Outputs:
- query_grad: bfloat16 [2, 2048, 1024], P('dp', 'seq')
- key_grad: bfloat16 [2, 2048, 1024], P('dp', 'seq')
- value_grad: bfloat16 [2, 2048, 1024], P('dp', 'seq')
- query_gain_grad: float32 [1024], replicated
- key_gain_grad: float32 [1024], replicated
The draws below stay inside these ranges and needn't reach their ends.
All inputs are finite; a program needn't handle non-finite values.
Results may differ from the reference program's by a relative error of at most 0.0065.
Values sent between devices are 32-bit elements; how exact they have to be, the bound alone decides.
A program may use at most 64 MiB of HBM per device.

```python
import math
import jax
import jax.numpy as jnp
from jax import lax

HEADS = 16
HEAD_DIM = 64
TOK_DEV = 128
LENGTH = 2048
BATCH = 2


def levels(key, shape, split, least, high):
    loudness = 1.0
    for axis_at, parts in split:
        heights = jax.random.uniform(jax.random.fold_in(jax.random.fold_in(key, 6), axis_at), (parts,), jnp.float32, least / len(split), high / len(split))
        loudness = loudness * jnp.repeat(jnp.exp(heights), shape[axis_at] // parts).reshape((-1,) + (1,) * (len(shape) - 1 - axis_at))
    return loudness


def bell_draw(rng, shape, deviation, most, cuts=(), kind=jnp.bfloat16):
    gain = levels(rng, shape, cuts, -0.22, 0.18) if cuts else 1.0
    entries = jax.random.normal(rng, shape, jnp.float32) * deviation * gain
    return jnp.minimum(jnp.maximum(entries, -most), most).astype(kind)


def setup_inputs(seed: int = 0) -> dict:
    seeds = jax.random.split(jax.random.key(seed), 7)
    query_rows = bell_draw(seeds[0], (BATCH, LENGTH, HEADS * HEAD_DIM), 1.0, 6.0, ((0, 2), (1, 16)))
    key_rows = bell_draw(seeds[1], (BATCH, LENGTH, HEADS * HEAD_DIM), 1.0, 6.0, ((0, 2), (1, 16)))
    value_rows = bell_draw(seeds[2], (BATCH, LENGTH, HEADS * HEAD_DIM), 1.0, 6.0, ((0, 2), (1, 16)))
    out_grad = bell_draw(seeds[3], (BATCH, LENGTH, HEADS * HEAD_DIM), 1.0, 6.0, ((0, 2), (1, 16)))
    query_gain = jnp.clip(1.0 + 0.18 * jax.random.normal(seeds[4], (HEADS * HEAD_DIM,), jnp.float32), 0.1, 1.9)
    key_gain = jnp.clip(1.0 + 0.18 * jax.random.normal(seeds[5], (HEADS * HEAD_DIM,), jnp.float32), 0.1, 1.9)
    return {"query_rows": query_rows, "key_rows": key_rows, "value_rows": value_rows, "out_grad": out_grad, "query_gain": query_gain, "key_gain": key_gain}


def one_sequence(items, query_gain, key_gain):
    queries, keys_in, value_inputs, grads = items
    nblk = LENGTH // TOK_DEV
    score_scale = 1.0 / math.sqrt(HEAD_DIM * LENGTH)

    def split_rows(x):
        return x.reshape(nblk, TOK_DEV, HEADS, HEAD_DIM).astype(jnp.float32)
    gained_q = (queries.astype(jnp.float32) * query_gain).astype(jnp.bfloat16)
    gained_k = (keys_in.astype(jnp.float32) * key_gain).astype(jnp.bfloat16)
    query_suffix = split_rows(gained_q)
    key_suffix = split_rows(gained_k)
    value_suffix = split_rows(value_inputs)
    output_grad_suffix = split_rows(grads)
    local_scores = jnp.einsum('xabg,xaby->xbgy', key_suffix, value_suffix)
    own_b = jnp.einsum('xabg,xaby->xbgy', query_suffix, output_grad_suffix)
    prefix_a = jnp.cumsum(local_scores, axis=0) - local_scores
    suffix_state = jnp.flip(jnp.cumsum(jnp.flip(own_b, 0), axis=0), 0) - own_b
    prefix_a = lax.optimization_barrier(prefix_a.astype(jnp.bfloat16)).astype(jnp.float32)
    suffix_state = lax.optimization_barrier(suffix_state.astype(jnp.bfloat16)).astype(jnp.float32)
    causal_masked = jnp.tril(jnp.ones((TOK_DEV, TOK_DEV), jnp.float32))
    pairwise_grad = jnp.einsum('ufwd,uiwd->uwfi', output_grad_suffix, value_suffix) * causal_masked
    pairwise_grad = lax.optimization_barrier(pairwise_grad.astype(jnp.bfloat16)).astype(jnp.float32)
    pair_score = jnp.einsum('nthd,nshd->nhts', query_suffix, key_suffix) * causal_masked
    pair_score = lax.optimization_barrier(pair_score.astype(jnp.bfloat16)).astype(jnp.float32)
    dq_gained = score_scale * (jnp.einsum('nhts,nshd->nthd', pairwise_grad, key_suffix) + jnp.einsum('nthe,nhde->nthd', output_grad_suffix, prefix_a))
    gained_key_grad = score_scale * (jnp.einsum('uaio,uiaf->uoaf', pairwise_grad, query_suffix) + jnp.einsum('zwyk,zypk->zwyp', value_suffix, suffix_state))
    dv = score_scale * (jnp.einsum('nhts,nthe->nshe', pair_score, output_grad_suffix) + jnp.einsum('nshd,nhde->nshe', key_suffix, suffix_state))
    dq_flat = dq_gained.reshape(LENGTH, HEADS * HEAD_DIM)
    dk_flat = gained_key_grad.reshape(LENGTH, HEADS * HEAD_DIM)
    query_grad = (dq_flat * query_gain).astype(jnp.bfloat16)
    key_grad = (dk_flat * key_gain).astype(jnp.bfloat16)
    value_grad = dv.reshape(LENGTH, HEADS * HEAD_DIM).astype(jnp.bfloat16)
    q_part = lax.optimization_barrier(jnp.sum(dq_flat * queries.astype(jnp.float32), axis=0))
    k_part = lax.optimization_barrier(jnp.sum(dk_flat * keys_in.astype(jnp.float32), axis=0))
    return (query_grad, key_grad, value_grad, q_part, k_part)

def reference(query_rows, key_rows, value_rows, out_grad, query_gain, key_gain):

    def apply(items):
        return one_sequence(items, query_gain, key_gain)
    query_grad, key_grad, value_grad, q_parts, k_parts = lax.map(apply, (query_rows, key_rows, value_rows, out_grad))
    factor = 1.0 / math.sqrt(BATCH * LENGTH)
    query_gain_grad = lax.optimization_barrier(jnp.sum(q_parts, axis=0)) * factor
    key_gain_grad = lax.optimization_barrier(jnp.sum(k_parts, axis=0)) * factor
    return (query_grad, key_grad, value_grad, query_gain_grad, key_gain_grad)
```

```python
import functools
import math

import jax
import jax.numpy as jnp
from jax import lax
from jax.experimental import pallas as pl
from jax.experimental.pallas import tpu as pltpu
from jax.sharding import PartitionSpec as P

HEADS = 16
HEAD_DIM = 64
PLANE = 4
MESH = pl.DeviceIdType.MESH
F32 = jnp.float32
BF16 = jnp.bfloat16
LANES = 2 * HEAD_DIM
PAIRS = HEADS // 2
CHUNKS = PAIRS // PLANE


def dot(a, b, da, db):
    return lax.dot_general(a, b, (((da,), (db,)), ((), ())), preferred_element_type=F32)


def kernel(n, ndp, rows, score_scale, factor, q_h, k_h, v_h, g_h, gain_q, gain_k,
           qo, ko, vo, gqo, gko,
           qx, kx, vx, gx, gq, gk, dqs, dks, dvs,
           own, rx1, zs, zr, exc, tx2, rx2, gtx, grx,
           in_sem, s1, r1, sz, rz, s2, r2, sg, rg):
    nz = n // PLANE
    dists = []
    d = 1
    while d < nz:
        dists.append(d)
        d *= 2
    me = lax.axis_index("seq")
    dp = lax.axis_index("dp")
    z = me // PLANE
    slot = me % PLANE
    x = slot % 2
    y = slot // 2
    fx = 1 - 2 * x
    fy = 2 - 4 * y
    hops = [fx, fy, fx + fy]

    loads = []
    for i, (src, dst) in enumerate(((k_h, kx), (v_h, vx), (q_h, qx), (g_h, gx))):
        cp = pltpu.make_async_copy(src.at[0], dst, in_sem.at[i])
        cp.start()
        loads.append(cp)

    barrier = pltpu.get_barrier_semaphore()

    def greet(**where):
        pl.semaphore_signal(barrier, inc=1, device_id=where, device_id_type=MESH)

    for h in hops:
        greet(seq=me + h)
    for d in dists:
        @pl.when(z + d < nz)
        def _(d=d):
            greet(seq=me + d * PLANE)

        @pl.when(z >= d)
        def _(d=d):
            greet(seq=me - d * PLANE)
    dp_bits = []
    d = 1
    while d < ndp:
        dp_bits.append(d)
        d *= 2
    for d in dp_bits:
        greet(dp=dp + d * (1 - 2 * ((dp // d) % 2)))

    lane = lax.broadcasted_iota(jnp.int32, (1, LANES), 1)
    first = (lane < HEAD_DIM).astype(F32).astype(BF16)
    second = (lane >= HEAD_DIM).astype(F32).astype(BF16)
    left = lax.broadcasted_iota(jnp.int32, (HEAD_DIM, LANES), 1) < HEAD_DIM

    def stack(t):
        return jnp.concatenate([t * first, t * second], axis=0)

    def cols(pair):
        return pl.ds(pair * LANES, LANES)

    def fold(full):
        return jnp.where(left, full[:HEAD_DIM], full[HEAD_DIM:])

    def copy1(c, h, hop):
        return pltpu.make_async_remote_copy(
            src_ref=own.at[c, slot + hop], dst_ref=rx1.at[c, slot],
            send_sem=s1.at[c, h], recv_sem=r1.at[c, h],
            device_id={"seq": me + hop}, device_id_type=MESH)

    def copy2(c, h, hop):
        return pltpu.make_async_remote_copy(
            src_ref=tx2.at[c, slot + hop], dst_ref=rx2.at[c, slot],
            send_sem=s2.at[c, h], recv_sem=r2.at[c, h],
            device_id={"seq": me + hop}, device_id_type=MESH)

    def copyz(c, s, ab):
        to = me + dists[s] * PLANE if ab == 0 else me - dists[s] * PLANE
        return pltpu.make_async_remote_copy(
            src_ref=zs.at[s, c, ab], dst_ref=zr.at[s, c, ab],
            send_sem=sz.at[s, c, ab], recv_sem=rz.at[s, c, ab],
            device_id={"seq": to}, device_id_type=MESH)

    def sends(s, ab):
        return z + dists[s] < nz if ab == 0 else z >= dists[s]

    def takes(s, ab):
        return z >= dists[s] if ab == 0 else z + dists[s] < nz

    def own_states(c):
        for p in range(PLANE):
            pair = p * CHUNKS + c
            gkp = (kx[:, cols(pair)].astype(F32) * gain_k[pair:pair + 1, :]).astype(BF16)
            gk[:, cols(pair)] = gkp
            own[c, p, 0] = fold(dot(gkp, vx[:, cols(pair)], 0, 0))
        if c == 0:
            loads[2].wait()
            loads[3].wait()
        for p in range(PLANE):
            pair = p * CHUNKS + c
            gqp = (qx[:, cols(pair)].astype(F32) * gain_q[pair:pair + 1, :]).astype(BF16)
            gq[:, cols(pair)] = gqp
            own[c, p, 1] = fold(dot(gqp, gx[:, cols(pair)], 0, 0))

    loads[0].wait()
    loads[1].wait()
    for c in range(CHUNKS):
        own_states(c)
        if c == 0:
            count = len(hops) + len(dp_bits)
            for d in dists:
                count = count + (z + d < nz).astype(jnp.int32) + (z >= d).astype(jnp.int32)
            pl.semaphore_wait(barrier, count)
        for h in (2, 0, 1):
            copy1(c, h, hops[h]).start()
        rx1[c, slot] = own[c, slot]

    row = lax.broadcasted_iota(jnp.int32, (rows, 2 * rows), 0)
    col = lax.broadcasted_iota(jnp.int32, (rows, 2 * rows), 1) % rows
    low = row >= col
    high = col >= row

    def intra(pair):
        sl = cols(pair)
        gv, vv, qv, kv = gx[:, sl], vx[:, sl], gq[:, sl], gk[:, sl]
        gs, qs = stack(gv), stack(qv)
        pg = jnp.where(low, dot(gv, stack(vv), 1, 1), 0.0).astype(BF16)
        dqs[:, sl] = dot(pg, stack(kv), 1, 0)
        pgt = jnp.where(high, dot(vv, gs, 1, 1), 0.0).astype(BF16)
        dks[:, sl] = dot(pgt, qs, 1, 0)
        pst = jnp.where(high, dot(kv, qs, 1, 1), 0.0).astype(BF16)
        dvs[:, sl] = dot(pst, gs, 1, 0)

    for pair in range(PAIRS):
        intra(pair)

    for c in range(CHUNKS):
        for h in range(3):
            copy1(c, h, hops[h]).wait_recv()
        zs[0, c] = (rx1[c, 0] + rx1[c, 1]) + (rx1[c, 2] + rx1[c, 3])
        exc[c] = jnp.zeros_like(exc[c])
        for ab in range(2):
            if dists:
                @pl.when(sends(0, ab))
                def _():
                    copyz(c, 0, ab).start()

    for s in range(len(dists)):
        for c in range(CHUNKS):
            for ab in range(2):
                @pl.when(takes(s, ab))
                def _():
                    copyz(c, s, ab).wait_recv()
                    got = zr[s, c, ab]
                    exc[c, ab] = exc[c, ab] + got
                    if s + 1 < len(dists):
                        zs[s + 1, c, ab] = zs[s, c, ab] + got
                if s + 1 < len(dists):
                    @pl.when(jnp.logical_not(takes(s, ab)))
                    def _():
                        zs[s + 1, c, ab] = zs[s, c, ab]

                    @pl.when(sends(s + 1, ab))
                    def _():
                        copyz(c, s + 1, ab).start()

    for c in range(CHUNKS):
        run = exc[c, 0]
        for p in range(PLANE):
            tx2[c, p, 0] = run
            if p + 1 < PLANE:
                run = run + rx1[c, p, 0]
        run = exc[c, 1]
        for p in reversed(range(PLANE)):
            tx2[c, p, 1] = run
            if p > 0:
                run = run + rx1[c, p, 1]
        for h in (2, 0, 1):
            copy2(c, h, hops[h]).start()
        rx2[c, slot] = tx2[c, slot]

    for c in range(CHUNKS):
        for h in range(3):
            copy2(c, h, hops[h]).wait_recv()
        for p in range(PLANE):
            pair = p * CHUNKS + c
            sl = cols(pair)
            sa = stack(rx2[c, p, 0].astype(BF16))
            sb = stack(rx2[c, p, 1].astype(BF16))
            dq = score_scale * (dqs[:, sl] + dot(gx[:, sl], sa, 1, 1))
            dk = score_scale * (dks[:, sl] + dot(vx[:, sl], sb, 1, 1))
            dv = score_scale * (dvs[:, sl] + dot(gk[:, sl], sb, 1, 0))
            qo[0, :, sl] = (dq * gain_q[pair:pair + 1, :]).astype(BF16)
            ko[0, :, sl] = (dk * gain_k[pair:pair + 1, :]).astype(BF16)
            vo[0, :, sl] = dv.astype(BF16)
            gtx[0, 0, pair:pair + 1, :] = jnp.sum(dq * qx[:, sl].astype(F32), axis=0, keepdims=True)
            gtx[0, 1, pair:pair + 1, :] = jnp.sum(dk * kx[:, sl].astype(F32), axis=0, keepdims=True)

    partners = [{"dp": dp + d * (1 - 2 * ((dp // d) % 2))} for d in dp_bits]
    d = 1
    while d < n:
        partners.append({"seq": me + d * (1 - 2 * ((me // d) % 2))})
        d *= 2

    def copyg(i):
        return pltpu.make_async_remote_copy(
            src_ref=gtx.at[i], dst_ref=grx.at[i], send_sem=sg.at[i], recv_sem=rg.at[i],
            device_id=partners[i], device_id_type=MESH)

    for i in range(len(partners)):
        copyg(i).start()
        copyg(i).wait_recv()
        gtx[i + 1] = gtx[i] + grx[i]
    last = len(partners)
    gqo[...] = gtx[last, 0] * factor
    gko[...] = gtx[last, 1] * factor

    for c in range(CHUNKS):
        for h in range(3):
            copy1(c, h, hops[h]).wait_send()
            copy2(c, h, hops[h]).wait_send()
        for s in range(len(dists)):
            for ab in range(2):
                @pl.when(sends(s, ab))
                def _():
                    copyz(c, s, ab).wait_send()
    for i in range(len(partners)):
        copyg(i).wait_send()


def solution(mesh):
    n = mesh.shape["seq"]
    ndp = mesh.shape["dp"]
    steps = max(1, (n // PLANE - 1).bit_length())
    gsteps = (n - 1).bit_length() + (ndp - 1).bit_length()

    def local(query_rows, key_rows, value_rows, out_grad, query_gain, key_gain):
        rows, width = query_rows.shape[1:]
        seq_len = rows * n
        score_scale = 1.0 / math.sqrt(HEAD_DIM * seq_len)
        factor = 1.0 / math.sqrt(seq_len * ndp)
        big = jax.ShapeDtypeStruct(query_rows.shape, BF16)
        small = jax.ShapeDtypeStruct((PAIRS, LANES), F32)
        vm = pl.BlockSpec(memory_space=pltpu.VMEM)
        hbm = pl.BlockSpec(memory_space=pltpu.HBM)
        unit = (2, HEAD_DIM, LANES)
        dma = pltpu.SemaphoreType.DMA
        out = pl.pallas_call(
            functools.partial(kernel, n, ndp, rows, score_scale, factor),
            out_shape=[big, big, big, small, small],
            in_specs=[hbm] * 4 + [vm] * 2,
            out_specs=[vm] * 5,
            scratch_shapes=[pltpu.VMEM((rows, width), BF16)] * 6
            + [pltpu.VMEM((rows, width), F32)] * 3
            + [
                pltpu.VMEM((CHUNKS, PLANE) + unit, F32),
                pltpu.VMEM((CHUNKS, PLANE) + unit, F32),
                pltpu.VMEM((steps, CHUNKS) + unit, F32),
                pltpu.VMEM((steps, CHUNKS) + unit, F32),
                pltpu.VMEM((CHUNKS,) + unit, F32),
                pltpu.VMEM((CHUNKS, PLANE) + unit, F32),
                pltpu.VMEM((CHUNKS, PLANE) + unit, F32),
                pltpu.VMEM((gsteps + 1, 2, PAIRS, LANES), F32),
                pltpu.VMEM((gsteps, 2, PAIRS, LANES), F32),
                dma((4,)),
                dma((CHUNKS, 3)), dma((CHUNKS, 3)),
                dma((steps, CHUNKS, 2)), dma((steps, CHUNKS, 2)),
                dma((CHUNKS, 3)), dma((CHUNKS, 3)),
                dma((gsteps,)), dma((gsteps,)),
            ],
            compiler_params=pltpu.CompilerParams(
                collective_id=0, has_side_effects=True, vmem_limit_bytes=32 * 1024 * 1024
            ),
        )(query_rows, key_rows, value_rows, out_grad,
          query_gain.reshape(PAIRS, LANES), key_gain.reshape(PAIRS, LANES))
        return (out[0], out[1], out[2], out[3].reshape(width), out[4].reshape(width))

    spec = P("dp", "seq", None)
    return jax.shard_map(local, mesh=mesh, in_specs=(spec,) * 4 + (P(), P()),
                         out_specs=(spec, spec, spec, P(), P()), check_vma=False)
```

```python
import functools
import math

import jax
import jax.numpy as jnp
from jax import lax
from jax.experimental import pallas as pl
from jax.experimental.pallas import tpu as pltpu
from jax.sharding import PartitionSpec as P

HEADS = 16
HEAD_DIM = 64
PLANE = 4
MESH = pl.DeviceIdType.MESH
F32 = jnp.float32
BF16 = jnp.bfloat16
LANES = 2 * HEAD_DIM
PAIRS = HEADS // 2
CHUNKS = PAIRS // PLANE
VMEM_BYTES = 60 * 1024 * 1024


def dot(a, b, da, db):
    return lax.dot_general(a, b, (((da,), (db,)), ((), ())), preferred_element_type=F32)


def kernel(n, ndp, rows, score_scale, factor, q_h, k_h, v_h, g_h, gq_h, gk_h,
           qo, ko, vo, gqo, gko,
           qx, kx, vx, gx, gq, gk, qb, kb, vb, gain_q, gain_k, gqb, gkb, dqs, dks, dvs,
           own, rx1, zs, zr, exc, tx2, rx2, gtx, grx,
           in_sem, gain_sem, out_sem, gout_sem, s1, r1, sz, rz, s2, r2, sg, rg):
    nz = n // PLANE
    dists = []
    d = 1
    while d < nz:
        dists.append(d)
        d *= 2
    me = lax.axis_index("seq")
    dp = lax.axis_index("dp")
    z = me // PLANE
    slot = me % PLANE
    x = slot % 2
    y = slot // 2
    fx = 1 - 2 * x
    fy = 2 - 4 * y
    hops = [fx, fy, fx + fy]

    span = PLANE * LANES

    def part(c):
        return pl.ds(c * span, span)

    gains = []
    for i, (src, dst) in enumerate(((gk_h, gain_k), (gq_h, gain_q))):
        gains.append(pltpu.make_async_copy(src, dst, gain_sem.at[i]))
        gains[i].start()
    loads = {}
    for c in range(CHUNKS):
        for i, (src, dst) in enumerate(((k_h, kx), (v_h, vx), (q_h, qx), (g_h, gx))):
            loads[c, i] = pltpu.make_async_copy(
                src.at[0, :, part(c)], dst.at[:, part(c)], in_sem.at[c, i])
            loads[c, i].start()

    barrier = pltpu.get_barrier_semaphore()

    def greet(**where):
        pl.semaphore_signal(barrier, inc=1, device_id=where, device_id_type=MESH)

    for h in hops:
        greet(seq=me + h)
    for d in dists:
        @pl.when(z + d < nz)
        def _(d=d):
            greet(seq=me + d * PLANE)

        @pl.when(z >= d)
        def _(d=d):
            greet(seq=me - d * PLANE)
    dp_bits = []
    d = 1
    while d < ndp:
        dp_bits.append(d)
        d *= 2
    for d in dp_bits:
        greet(dp=dp + d * (1 - 2 * ((dp // d) % 2)))

    lane = lax.broadcasted_iota(jnp.int32, (1, LANES), 1)
    first = (lane < HEAD_DIM).astype(F32).astype(BF16)
    second = (lane >= HEAD_DIM).astype(F32).astype(BF16)
    left = lax.broadcasted_iota(jnp.int32, (HEAD_DIM, LANES), 1) < HEAD_DIM

    def stack(t):
        return jnp.concatenate([t * first, t * second], axis=0)

    def cols(pair):
        return pl.ds(pair * LANES, LANES)

    def fold(full):
        return jnp.where(left, full[:HEAD_DIM], full[HEAD_DIM:])

    def copy1(c, h, hop):
        return pltpu.make_async_remote_copy(
            src_ref=own.at[c, slot + hop], dst_ref=rx1.at[c, slot],
            send_sem=s1.at[c, h], recv_sem=r1.at[c, h],
            device_id={"seq": me + hop}, device_id_type=MESH)

    def copy2(c, h, hop):
        return pltpu.make_async_remote_copy(
            src_ref=tx2.at[c, slot + hop], dst_ref=rx2.at[c, slot],
            send_sem=s2.at[c, h], recv_sem=r2.at[c, h],
            device_id={"seq": me + hop}, device_id_type=MESH)

    def copyz(c, s, ab):
        to = me + dists[s] * PLANE if ab == 0 else me - dists[s] * PLANE
        return pltpu.make_async_remote_copy(
            src_ref=zs.at[s, c, ab], dst_ref=zr.at[s, c, ab],
            send_sem=sz.at[s, c, ab], recv_sem=rz.at[s, c, ab],
            device_id={"seq": to}, device_id_type=MESH)

    def sends(s, ab):
        return z + dists[s] < nz if ab == 0 else z >= dists[s]

    def takes(s, ab):
        return z >= dists[s] if ab == 0 else z + dists[s] < nz

    def own_states(c):
        if c == 0:
            gains[0].wait()
        loads[c, 0].wait()
        loads[c, 1].wait()
        for p in range(PLANE):
            pair = c * PLANE + p
            gkp = (kx[:, cols(pair)].astype(F32) * gain_k[pair:pair + 1, :]).astype(BF16)
            gk[:, cols(pair)] = gkp
            own[c, p, 0] = fold(dot(gkp, vx[:, cols(pair)], 0, 0))
        if c == 0:
            gains[1].wait()
        loads[c, 2].wait()
        loads[c, 3].wait()
        for p in range(PLANE):
            pair = c * PLANE + p
            gqp = (qx[:, cols(pair)].astype(F32) * gain_q[pair:pair + 1, :]).astype(BF16)
            gq[:, cols(pair)] = gqp
            own[c, p, 1] = fold(dot(gqp, gx[:, cols(pair)], 0, 0))

    for c in range(CHUNKS):
        own_states(c)
        if c == 0:
            count = len(hops) + len(dp_bits)
            for d in dists:
                count = count + (z + d < nz).astype(jnp.int32) + (z >= d).astype(jnp.int32)
            pl.semaphore_wait(barrier, count)
        for h in (2, 0, 1):
            copy1(c, h, hops[h]).start()
        rx1[c, slot] = own[c, slot]

    row = lax.broadcasted_iota(jnp.int32, (rows, 2 * rows), 0)
    col = lax.broadcasted_iota(jnp.int32, (rows, 2 * rows), 1) % rows
    low = row >= col
    high = col >= row

    def intra(pair):
        sl = cols(pair)
        gv, vv, qv, kv = gx[:, sl], vx[:, sl], gq[:, sl], gk[:, sl]
        gs, qs = stack(gv), stack(qv)
        pg = jnp.where(low, dot(gv, stack(vv), 1, 1), 0.0).astype(BF16)
        dq = score_scale * dot(pg, stack(kv), 1, 0)
        dqs[:, sl] = dq
        gtx[0, 0, pair:pair + 1, :] = jnp.sum(dq * qx[:, sl].astype(F32), axis=0, keepdims=True)
        pgt = jnp.where(high, dot(vv, gs, 1, 1), 0.0).astype(BF16)
        dk = score_scale * dot(pgt, qs, 1, 0)
        dks[:, sl] = dk
        gtx[0, 1, pair:pair + 1, :] = jnp.sum(dk * kx[:, sl].astype(F32), axis=0, keepdims=True)
        pst = jnp.where(high, dot(kv, qs, 1, 1), 0.0).astype(BF16)
        dvs[:, sl] = score_scale * dot(pst, gs, 1, 0)

    steps = len(dists)

    def totals(c):
        for h in range(3):
            copy1(c, h, hops[h]).wait_recv()
        zs[0, c] = (rx1[c, 0] + rx1[c, 1]) + (rx1[c, 2] + rx1[c, 3])
        exc[c] = jnp.zeros_like(exc[c])
        for ab in range(2):
            if dists:
                @pl.when(sends(0, ab))
                def _():
                    copyz(c, 0, ab).start()

    def scan(s, c):
        for ab in range(2):
            @pl.when(takes(s, ab))
            def _():
                copyz(c, s, ab).wait_recv()
                got = zr[s, c, ab]
                exc[c, ab] = exc[c, ab] + got
                if s + 1 < steps:
                    zs[s + 1, c, ab] = zs[s, c, ab] + got
            if s + 1 < steps:
                @pl.when(jnp.logical_not(takes(s, ab)))
                def _():
                    zs[s + 1, c, ab] = zs[s, c, ab]

                @pl.when(sends(s + 1, ab))
                def _():
                    copyz(c, s + 1, ab).start()

    def give(c):
        run = exc[c, 0]
        both = jnp.zeros_like(run)
        for p in range(PLANE):
            tx2[c, p, 0] = run
            both = both + run * rx1[c, p, 1]
            if p + 1 < PLANE:
                run = run + rx1[c, p, 0]
        run = exc[c, 1]
        for p in reversed(range(PLANE)):
            tx2[c, p, 1] = run
            if p > 0:
                run = run + rx1[c, p, 1]
        for h in (2, 0, 1):
            copy2(c, h, hops[h]).start()
        rx2[c, slot] = tx2[c, slot]
        spread = jnp.concatenate([jnp.where(left, both, 0.0), jnp.where(left, 0.0, both)], axis=0)
        line = lax.dot_general(
            jnp.ones((8, LANES), F32), spread, (((1,), (1,)), ((), ())),
            precision=lax.Precision.HIGHEST, preferred_element_type=F32)
        gtx[0, 2, pl.ds(c * PLANE + slot, 1), :] = line[:1] * score_scale

    def final(c):
        for h in range(3):
            copy2(c, h, hops[h]).wait_recv()
        for p in range(PLANE):
            pair = c * PLANE + p
            sl = cols(pair)
            sa = stack(rx2[c, p, 0].astype(BF16))
            sb = stack(rx2[c, p, 1].astype(BF16))
            dq = dqs[:, sl] + score_scale * dot(gx[:, sl], sa, 1, 1)
            dk = dks[:, sl] + score_scale * dot(vx[:, sl], sb, 1, 1)
            dv = dvs[:, sl] + score_scale * dot(gk[:, sl], sb, 1, 0)
            qb[:, sl] = (dq * gain_q[pair:pair + 1, :]).astype(BF16)
            kb[:, sl] = (dk * gain_k[pair:pair + 1, :]).astype(BF16)
            vb[:, sl] = dv.astype(BF16)
        for i in range(3):
            stores(c, i).start()

    def stores(c, i):
        src, dst = ((qb, qo), (kb, ko), (vb, vo))[i]
        return pltpu.make_async_copy(src.at[:, part(c)], dst.at[0, :, part(c)], out_sem.at[c, i])

    gtx[0, 2] = jnp.zeros((PAIRS, LANES), F32)
    todo = list(range(PAIRS))

    def fill(count):
        for _ in range(min(count, len(todo))):
            intra(todo.pop(0))

    for c in range(CHUNKS):
        fill(3)
        totals(c)
    for s in range(steps):
        for c in range(CHUNKS):
            if s == 0:
                fill(1)
            scan(s, c)
            if s + 1 == steps:
                fill(PAIRS)
                give(c)
    if not steps:
        fill(PAIRS)
        for c in range(CHUNKS):
            give(c)

    partners = [{"dp": dp + d * (1 - 2 * ((dp // d) % 2))} for d in dp_bits]
    for d in [d * PLANE for d in dists] + [1, 2]:
        partners.append({"seq": me + d * (1 - 2 * ((me // d) % 2))})

    def copyg(i):
        return pltpu.make_async_remote_copy(
            src_ref=gtx.at[i], dst_ref=grx.at[i], send_sem=sg.at[i], recv_sem=rg.at[i],
            device_id=partners[i], device_id_type=MESH)

    last = len(partners)
    when = {last - 2 - (CHUNKS - 1 - c): c for c in range(CHUNKS - 1)}
    for i in range(last):
        copyg(i).start()
        if i in when:
            final(when[i])
        copyg(i).wait_recv()
        gtx[i + 1] = gtx[i] + grx[i]
    gqb[...] = (gtx[last, 0] + gtx[last, 2] / gain_q[...]) * factor
    gkb[...] = (gtx[last, 1] + gtx[last, 2] / gain_k[...]) * factor
    gout = [pltpu.make_async_copy(gqb, gqo, gout_sem.at[0]),
            pltpu.make_async_copy(gkb, gko, gout_sem.at[1])]
    for cp in gout:
        cp.start()
    final(CHUNKS - 1)

    for c in range(CHUNKS):
        for h in range(3):
            copy1(c, h, hops[h]).wait_send()
            copy2(c, h, hops[h]).wait_send()
        for s in range(len(dists)):
            for ab in range(2):
                @pl.when(sends(s, ab))
                def _():
                    copyz(c, s, ab).wait_send()
    for i in range(last):
        copyg(i).wait_send()
    for cp in gout:
        cp.wait()
    for c in range(CHUNKS):
        for i in range(3):
            stores(c, i).wait()


def move(*refs):
    sem = refs[-1]
    half = (len(refs) - 1) // 2
    copies = [pltpu.make_async_copy(refs[i], refs[half + i], sem.at[i]) for i in range(half)]
    for cp in copies:
        cp.start()
    for cp in copies:
        cp.wait()


def solution(mesh):
    n = mesh.shape["seq"]
    ndp = mesh.shape["dp"]
    steps = max(1, (n // PLANE - 1).bit_length())
    gsteps = (n - 1).bit_length() + (ndp - 1).bit_length()

    def local(query_rows, key_rows, value_rows, out_grad, query_gain, key_gain):
        rows, width = query_rows.shape[1:]
        seq_len = rows * n
        score_scale = 1.0 / math.sqrt(HEAD_DIM * seq_len)
        factor = 1.0 / math.sqrt(seq_len * ndp)
        big = jax.ShapeDtypeStruct(query_rows.shape, BF16)
        small = jax.ShapeDtypeStruct((PAIRS, LANES), F32)
        hbm = pl.BlockSpec(memory_space=pltpu.HBM)
        unit = (2, HEAD_DIM, LANES)
        dma = pltpu.SemaphoreType.DMA
        out = pl.pallas_call(
            functools.partial(kernel, n, ndp, rows, score_scale, factor),
            out_shape=[big, big, big, small, small],
            in_specs=[hbm] * 6,
            out_specs=[hbm] * 5,
            scratch_shapes=[pltpu.VMEM((rows, width), BF16)] * 9
            + [pltpu.VMEM((PAIRS, LANES), F32)] * 4
            + [pltpu.VMEM((rows, width), F32)] * 3
            + [
                pltpu.VMEM((CHUNKS, PLANE) + unit, F32),
                pltpu.VMEM((CHUNKS, PLANE) + unit, F32),
                pltpu.VMEM((steps, CHUNKS) + unit, F32),
                pltpu.VMEM((steps, CHUNKS) + unit, F32),
                pltpu.VMEM((CHUNKS,) + unit, F32),
                pltpu.VMEM((CHUNKS, PLANE) + unit, F32),
                pltpu.VMEM((CHUNKS, PLANE) + unit, F32),
                pltpu.VMEM((gsteps + 1, 3, PAIRS, LANES), F32),
                pltpu.VMEM((gsteps, 3, PAIRS, LANES), F32),
                dma((CHUNKS, 4)), dma((2,)), dma((CHUNKS, 3)), dma((2,)),
                dma((CHUNKS, 3)), dma((CHUNKS, 3)),
                dma((steps, CHUNKS, 2)), dma((steps, CHUNKS, 2)),
                dma((CHUNKS, 3)), dma((CHUNKS, 3)),
                dma((gsteps,)), dma((gsteps,)),
            ],
            compiler_params=pltpu.CompilerParams(
                collective_id=0, has_side_effects=True, vmem_limit_bytes=VMEM_BYTES
            ),
        )(query_rows, key_rows, value_rows, out_grad,
          query_gain.reshape(PAIRS, LANES), key_gain.reshape(PAIRS, LANES))
        out = pl.pallas_call(
            move,
            out_shape=[big, big, big, small, small],
            in_specs=[hbm] * 5,
            out_specs=[hbm] * 5,
            scratch_shapes=[dma((5,))],
            compiler_params=pltpu.CompilerParams(vmem_limit_bytes=VMEM_BYTES),
        )(*out)
        return (out[0], out[1], out[2], out[3].reshape(width), out[4].reshape(width))

    spec = P("dp", "seq", None)
    return jax.shard_map(local, mesh=mesh, in_specs=(spec,) * 4 + (P(), P()),
                         out_specs=(spec, spec, spec, P(), P()), check_vma=False)
```

```python
import functools
import math

import jax
import jax.numpy as jnp
from jax import lax
from jax.experimental import pallas as pl
from jax.experimental.pallas import tpu as pltpu
from jax.sharding import PartitionSpec as P

HEADS = 16
HEAD_DIM = 64
PLANE = 4
MESH = pl.DeviceIdType.MESH
F32 = jnp.float32
BF16 = jnp.bfloat16
LANES = 2 * HEAD_DIM
PAIRS = HEADS // 2
CHUNKS = PAIRS // PLANE


def dot(a, b, da, db):
    return lax.dot_general(a, b, (((da,), (db,)), ((), ())), preferred_element_type=F32)


def kernel(n, ndp, rows, score_scale, factor, q_h, k_h, v_h, g_h, gq_h, gk_h,
           qo, ko, vo, gqo, gko,
           qx, kx, vx, gx, gq, gk, gain_q, gain_k, dqs, dks, dvs,
           own, rx1, zs, zr, exc, tx2, rx2, gtx, grx,
           in_sem, gain_sem, s1, r1, sz, rz, s2, r2, sg, rg):
    nz = n // PLANE
    dists = []
    d = 1
    while d < nz:
        dists.append(d)
        d *= 2
    me = lax.axis_index("seq")
    dp = lax.axis_index("dp")
    z = me // PLANE
    slot = me % PLANE
    x = slot % 2
    y = slot // 2
    fx = 1 - 2 * x
    fy = 2 - 4 * y
    hops = [fx, fy, fx + fy]

    span = PLANE * LANES

    def part(c):
        return pl.ds(c * span, span)

    gains = []
    for i, (src, dst) in enumerate(((gk_h, gain_k), (gq_h, gain_q))):
        gains.append(pltpu.make_async_copy(src, dst, gain_sem.at[i]))
        gains[i].start()
    loads = {}
    for c in range(CHUNKS):
        for i, (src, dst) in enumerate(((k_h, kx), (v_h, vx), (q_h, qx), (g_h, gx))):
            loads[c, i] = pltpu.make_async_copy(
                src.at[0, :, part(c)], dst.at[:, part(c)], in_sem.at[c, i])
            loads[c, i].start()

    barrier = pltpu.get_barrier_semaphore()

    def greet(**where):
        pl.semaphore_signal(barrier, inc=1, device_id=where, device_id_type=MESH)

    for h in hops:
        greet(seq=me + h)
    for d in dists:
        @pl.when(z + d < nz)
        def _(d=d):
            greet(seq=me + d * PLANE)

        @pl.when(z >= d)
        def _(d=d):
            greet(seq=me - d * PLANE)
    dp_bits = []
    d = 1
    while d < ndp:
        dp_bits.append(d)
        d *= 2
    for d in dp_bits:
        greet(dp=dp + d * (1 - 2 * ((dp // d) % 2)))

    lane = lax.broadcasted_iota(jnp.int32, (1, LANES), 1)
    first = (lane < HEAD_DIM).astype(F32).astype(BF16)
    second = (lane >= HEAD_DIM).astype(F32).astype(BF16)
    left = lax.broadcasted_iota(jnp.int32, (HEAD_DIM, LANES), 1) < HEAD_DIM

    def stack(t):
        return jnp.concatenate([t * first, t * second], axis=0)

    def cols(pair):
        return pl.ds(pair * LANES, LANES)

    def fold(full):
        return jnp.where(left, full[:HEAD_DIM], full[HEAD_DIM:])

    def copy1(c, h, hop):
        return pltpu.make_async_remote_copy(
            src_ref=own.at[c, slot + hop], dst_ref=rx1.at[c, slot],
            send_sem=s1.at[c, h], recv_sem=r1.at[c, h],
            device_id={"seq": me + hop}, device_id_type=MESH)

    def copy2(c, h, hop):
        return pltpu.make_async_remote_copy(
            src_ref=tx2.at[c, slot + hop], dst_ref=rx2.at[c, slot],
            send_sem=s2.at[c, h], recv_sem=r2.at[c, h],
            device_id={"seq": me + hop}, device_id_type=MESH)

    def copyz(c, s, ab):
        to = me + dists[s] * PLANE if ab == 0 else me - dists[s] * PLANE
        return pltpu.make_async_remote_copy(
            src_ref=zs.at[s, c, ab], dst_ref=zr.at[s, c, ab],
            send_sem=sz.at[s, c, ab], recv_sem=rz.at[s, c, ab],
            device_id={"seq": to}, device_id_type=MESH)

    def sends(s, ab):
        return z + dists[s] < nz if ab == 0 else z >= dists[s]

    def takes(s, ab):
        return z >= dists[s] if ab == 0 else z + dists[s] < nz

    def own_states(c):
        if c == 0:
            gains[0].wait()
        loads[c, 0].wait()
        loads[c, 1].wait()
        for p in range(PLANE):
            pair = c * PLANE + p
            gkp = (kx[:, cols(pair)].astype(F32) * gain_k[pair:pair + 1, :]).astype(BF16)
            gk[:, cols(pair)] = gkp
            own[c, p, 0] = fold(dot(gkp, vx[:, cols(pair)], 0, 0))
        if c == 0:
            gains[1].wait()
        loads[c, 2].wait()
        loads[c, 3].wait()
        for p in range(PLANE):
            pair = c * PLANE + p
            gqp = (qx[:, cols(pair)].astype(F32) * gain_q[pair:pair + 1, :]).astype(BF16)
            gq[:, cols(pair)] = gqp
            own[c, p, 1] = fold(dot(gqp, gx[:, cols(pair)], 0, 0))

    for c in range(CHUNKS):
        own_states(c)
        if c == 0:
            count = len(hops) + len(dp_bits)
            for d in dists:
                count = count + (z + d < nz).astype(jnp.int32) + (z >= d).astype(jnp.int32)
            pl.semaphore_wait(barrier, count)
        for h in (2, 0, 1):
            copy1(c, h, hops[h]).start()
        rx1[c, slot] = own[c, slot]

    row = lax.broadcasted_iota(jnp.int32, (rows, 2 * rows), 0)
    col = lax.broadcasted_iota(jnp.int32, (rows, 2 * rows), 1) % rows
    low = row >= col
    high = col >= row

    def intra(pair):
        sl = cols(pair)
        gv, vv, qv, kv = gx[:, sl], vx[:, sl], gq[:, sl], gk[:, sl]
        gs, qs = stack(gv), stack(qv)
        pg = jnp.where(low, dot(gv, stack(vv), 1, 1), 0.0).astype(BF16)
        dq = score_scale * dot(pg, stack(kv), 1, 0)
        dqs[:, sl] = dq
        gtx[0, 0, pair:pair + 1, :] = jnp.sum(dq * qx[:, sl].astype(F32), axis=0, keepdims=True)
        pgt = jnp.where(high, dot(vv, gs, 1, 1), 0.0).astype(BF16)
        dk = score_scale * dot(pgt, qs, 1, 0)
        dks[:, sl] = dk
        gtx[0, 1, pair:pair + 1, :] = jnp.sum(dk * kx[:, sl].astype(F32), axis=0, keepdims=True)
        pst = jnp.where(high, dot(kv, qs, 1, 1), 0.0).astype(BF16)
        dvs[:, sl] = score_scale * dot(pst, gs, 1, 0)

    steps = len(dists)

    def totals(c):
        for h in range(3):
            copy1(c, h, hops[h]).wait_recv()
        zs[0, c] = (rx1[c, 0] + rx1[c, 1]) + (rx1[c, 2] + rx1[c, 3])
        exc[c] = jnp.zeros_like(exc[c])
        for ab in range(2):
            if dists:
                @pl.when(sends(0, ab))
                def _():
                    copyz(c, 0, ab).start()

    def scan(s, c):
        for ab in range(2):
            @pl.when(takes(s, ab))
            def _():
                copyz(c, s, ab).wait_recv()
                got = zr[s, c, ab]
                exc[c, ab] = exc[c, ab] + got
                if s + 1 < steps:
                    zs[s + 1, c, ab] = zs[s, c, ab] + got
            if s + 1 < steps:
                @pl.when(jnp.logical_not(takes(s, ab)))
                def _():
                    zs[s + 1, c, ab] = zs[s, c, ab]

                @pl.when(sends(s + 1, ab))
                def _():
                    copyz(c, s + 1, ab).start()

    def give(c):
        run = exc[c, 0]
        both = jnp.zeros_like(run)
        for p in range(PLANE):
            tx2[c, p, 0] = run
            both = both + run * rx1[c, p, 1]
            if p + 1 < PLANE:
                run = run + rx1[c, p, 0]
        run = exc[c, 1]
        for p in reversed(range(PLANE)):
            tx2[c, p, 1] = run
            if p > 0:
                run = run + rx1[c, p, 1]
        for h in (2, 0, 1):
            copy2(c, h, hops[h]).start()
        rx2[c, slot] = tx2[c, slot]
        spread = jnp.concatenate([jnp.where(left, both, 0.0), jnp.where(left, 0.0, both)], axis=0)
        line = lax.dot_general(
            jnp.ones((8, LANES), F32), spread, (((1,), (1,)), ((), ())),
            precision=lax.Precision.HIGHEST, preferred_element_type=F32)
        gtx[0, 2, pl.ds(c * PLANE + slot, 1), :] = line[:1] * score_scale

    def final(c):
        for h in range(3):
            copy2(c, h, hops[h]).wait_recv()
        for p in range(PLANE):
            pair = c * PLANE + p
            sl = cols(pair)
            sa = stack(rx2[c, p, 0].astype(BF16))
            sb = stack(rx2[c, p, 1].astype(BF16))
            dq = dqs[:, sl] + score_scale * dot(gx[:, sl], sa, 1, 1)
            dk = dks[:, sl] + score_scale * dot(vx[:, sl], sb, 1, 1)
            dv = dvs[:, sl] + score_scale * dot(gk[:, sl], sb, 1, 0)
            qo[0, :, sl] = (dq * gain_q[pair:pair + 1, :]).astype(BF16)
            ko[0, :, sl] = (dk * gain_k[pair:pair + 1, :]).astype(BF16)
            vo[0, :, sl] = dv.astype(BF16)

    gtx[0, 2] = jnp.zeros((PAIRS, LANES), F32)
    todo = list(range(PAIRS))

    def fill(count):
        for _ in range(min(count, len(todo))):
            intra(todo.pop(0))

    for c in range(CHUNKS):
        fill(3)
        totals(c)
    for s in range(steps):
        for c in range(CHUNKS):
            if s == 0:
                fill(1)
            scan(s, c)
            if s + 1 == steps:
                fill(PAIRS)
                give(c)
    if not steps:
        fill(PAIRS)
        for c in range(CHUNKS):
            give(c)

    partners = [{"dp": dp + d * (1 - 2 * ((dp // d) % 2))} for d in dp_bits]
    for d in [d * PLANE for d in dists] + [1, 2]:
        partners.append({"seq": me + d * (1 - 2 * ((me // d) % 2))})

    def copyg(i):
        return pltpu.make_async_remote_copy(
            src_ref=gtx.at[i], dst_ref=grx.at[i], send_sem=sg.at[i], recv_sem=rg.at[i],
            device_id=partners[i], device_id_type=MESH)

    last = len(partners)
    when = {last - 2 - (CHUNKS - 1 - c): c for c in range(CHUNKS - 1)}
    for i in range(last):
        copyg(i).start()
        if i in when:
            final(when[i])
        copyg(i).wait_recv()
        gtx[i + 1] = gtx[i] + grx[i]
    gqo[...] = (gtx[last, 0] + gtx[last, 2] / gain_q[...]) * factor
    gko[...] = (gtx[last, 1] + gtx[last, 2] / gain_k[...]) * factor
    final(CHUNKS - 1)

    for c in range(CHUNKS):
        for h in range(3):
            copy1(c, h, hops[h]).wait_send()
            copy2(c, h, hops[h]).wait_send()
        for s in range(len(dists)):
            for ab in range(2):
                @pl.when(sends(s, ab))
                def _():
                    copyz(c, s, ab).wait_send()
    for i in range(last):
        copyg(i).wait_send()


def move(*refs):
    sem = refs[-1]
    half = (len(refs) - 1) // 2
    copies = [pltpu.make_async_copy(refs[i], refs[half + i], sem.at[i]) for i in range(half)]
    for cp in copies:
        cp.start()
    for cp in copies:
        cp.wait()


def solution(mesh):
    n = mesh.shape["seq"]
    ndp = mesh.shape["dp"]
    steps = max(1, (n // PLANE - 1).bit_length())
    gsteps = (n - 1).bit_length() + (ndp - 1).bit_length()

    def local(query_rows, key_rows, value_rows, out_grad, query_gain, key_gain):
        rows, width = query_rows.shape[1:]
        seq_len = rows * n
        score_scale = 1.0 / math.sqrt(HEAD_DIM * seq_len)
        factor = 1.0 / math.sqrt(seq_len * ndp)
        big = jax.ShapeDtypeStruct(query_rows.shape, BF16)
        small = jax.ShapeDtypeStruct((PAIRS, LANES), F32)
        hbm = pl.BlockSpec(memory_space=pltpu.HBM)
        unit = (2, HEAD_DIM, LANES)
        dma = pltpu.SemaphoreType.DMA
        out = pl.pallas_call(
            functools.partial(kernel, n, ndp, rows, score_scale, factor),
            out_shape=[big, big, big, small, small],
            in_specs=[hbm] * 6,
            out_specs=[pl.BlockSpec(memory_space=pltpu.VMEM)] * 5,
            scratch_shapes=[pltpu.VMEM((rows, width), BF16)] * 6
            + [pltpu.VMEM((PAIRS, LANES), F32)] * 2
            + [pltpu.VMEM((rows, width), F32)] * 3
            + [
                pltpu.VMEM((CHUNKS, PLANE) + unit, F32),
                pltpu.VMEM((CHUNKS, PLANE) + unit, F32),
                pltpu.VMEM((steps, CHUNKS) + unit, F32),
                pltpu.VMEM((steps, CHUNKS) + unit, F32),
                pltpu.VMEM((CHUNKS,) + unit, F32),
                pltpu.VMEM((CHUNKS, PLANE) + unit, F32),
                pltpu.VMEM((CHUNKS, PLANE) + unit, F32),
                pltpu.VMEM((gsteps + 1, 3, PAIRS, LANES), F32),
                pltpu.VMEM((gsteps, 3, PAIRS, LANES), F32),
                dma((CHUNKS, 4)), dma((2,)),
                dma((CHUNKS, 3)), dma((CHUNKS, 3)),
                dma((steps, CHUNKS, 2)), dma((steps, CHUNKS, 2)),
                dma((CHUNKS, 3)), dma((CHUNKS, 3)),
                dma((gsteps,)), dma((gsteps,)),
            ],
            compiler_params=pltpu.CompilerParams(
                collective_id=0, has_side_effects=True, vmem_limit_bytes=32 * 1024 * 1024
            ),
        )(*[pltpu.with_memory_space_constraint(t, pltpu.HBM) for t in (
            query_rows, key_rows, value_rows, out_grad,
            query_gain.reshape(PAIRS, LANES), key_gain.reshape(PAIRS, LANES))])
        out = pl.pallas_call(
            move,
            out_shape=[big, big, big, small, small],
            in_specs=[pl.BlockSpec(memory_space=pltpu.VMEM)] * 5,
            out_specs=[hbm] * 5,
            scratch_shapes=[dma((5,))],
        )(*[pltpu.with_memory_space_constraint(t, pltpu.VMEM) for t in out])
        return (out[0], out[1], out[2], out[3].reshape(width), out[4].reshape(width))

    spec = P("dp", "seq", None)
    return jax.shard_map(local, mesh=mesh, in_specs=(spec,) * 4 + (P(), P()),
                         out_specs=(spec, spec, spec, P(), P()), check_vma=False)
```

```python
import functools
import math

import jax
import jax.numpy as jnp
from jax import lax
from jax.experimental import pallas as pl
from jax.experimental.pallas import tpu as pltpu
from jax.sharding import PartitionSpec as P

HEADS = 16
HEAD_DIM = 64
PLANE = 4
MESH = pl.DeviceIdType.MESH
F32 = jnp.float32
BF16 = jnp.bfloat16
LANES = 2 * HEAD_DIM
PAIRS = HEADS // 2
CHUNKS = PAIRS // PLANE


def dot(a, b, da, db):
    return lax.dot_general(a, b, (((da,), (db,)), ((), ())), preferred_element_type=F32)


def kernel(n, ndp, rows, score_scale, factor, q_h, k_h, v_h, g_h, gq_h, gk_h,
           qo, ko, vo, gqo, gko,
           qx, kx, vx, gx, gq, gk, gain_q, gain_k, dqs, dks, dvs,
           own, rx1, zs, zr, exc, tx2, rx2, gtx, grx, gpl,
           in_sem, gain_sem, s1, r1, sz, rz, s2, r2, sg, rg, sp, rp):
    nz = n // PLANE
    dists = []
    d = 1
    while d < nz:
        dists.append(d)
        d *= 2
    me = lax.axis_index("seq")
    dp = lax.axis_index("dp")
    z = me // PLANE
    slot = me % PLANE
    x = slot % 2
    y = slot // 2
    fx = 1 - 2 * x
    fy = 2 - 4 * y
    hops = [fx, fy, fx + fy]

    barrier = pltpu.get_barrier_semaphore()

    def greet(**where):
        pl.semaphore_signal(barrier, inc=1, device_id=where, device_id_type=MESH)

    for h in hops:
        greet(seq=me + h)
    for d in dists:
        @pl.when(z + d < nz)
        def _(d=d):
            greet(seq=me + d * PLANE)

        @pl.when(z >= d)
        def _(d=d):
            greet(seq=me - d * PLANE)
    dp_bits = []
    d = 1
    while d < ndp:
        dp_bits.append(d)
        d *= 2
    for d in dp_bits:
        greet(dp=dp + d * (1 - 2 * ((dp // d) % 2)))

    span = PLANE * LANES

    def part(c):
        return pl.ds(c * span, span)

    gains = []
    for i, (src, dst) in enumerate(((gk_h, gain_k), (gq_h, gain_q))):
        gains.append(pltpu.make_async_copy(src, dst, gain_sem.at[i]))
        gains[i].start()
    loads = {}
    for c in range(CHUNKS):
        for i, (src, dst) in enumerate(((k_h, kx), (v_h, vx), (q_h, qx), (g_h, gx))):
            loads[c, i] = pltpu.make_async_copy(
                src.at[0, :, part(c)], dst.at[:, part(c)], in_sem.at[c, i])
            loads[c, i].start()

    lane = lax.broadcasted_iota(jnp.int32, (1, LANES), 1)
    first = (lane < HEAD_DIM).astype(F32).astype(BF16)
    second = (lane >= HEAD_DIM).astype(F32).astype(BF16)
    left = lax.broadcasted_iota(jnp.int32, (HEAD_DIM, LANES), 1) < HEAD_DIM

    def stack(t):
        return jnp.concatenate([t * first, t * second], axis=0)

    def cols(pair):
        return pl.ds(pair * LANES, LANES)

    def fold(full):
        return jnp.where(left, full[:HEAD_DIM], full[HEAD_DIM:])

    def copy1(c, ab, h):
        hop = hops[h]
        return pltpu.make_async_remote_copy(
            src_ref=own.at[c, ab, slot + hop], dst_ref=rx1.at[c, ab, slot],
            send_sem=s1.at[c, ab, h], recv_sem=r1.at[c, ab, h],
            device_id={"seq": me + hop}, device_id_type=MESH)

    def copy2(c, ab, h):
        hop = hops[h]
        return pltpu.make_async_remote_copy(
            src_ref=tx2.at[c, ab, slot + hop], dst_ref=rx2.at[c, ab, slot],
            send_sem=s2.at[c, ab, h], recv_sem=r2.at[c, ab, h],
            device_id={"seq": me + hop}, device_id_type=MESH)

    def copyz(c, s, ab):
        to = me + dists[s] * PLANE if ab == 0 else me - dists[s] * PLANE
        return pltpu.make_async_remote_copy(
            src_ref=zs.at[s, c, ab], dst_ref=zr.at[s, c, ab],
            send_sem=sz.at[s, c, ab], recv_sem=rz.at[s, c, ab],
            device_id={"seq": to}, device_id_type=MESH)

    def sends(s, ab):
        return z + dists[s] < nz if ab == 0 else z >= dists[s]

    def takes(s, ab):
        return z >= dists[s] if ab == 0 else z + dists[s] < nz

    def own_state(c, ab):
        raw, gain, mult, other = ((kx, gain_k, gk, vx), (qx, gain_q, gq, gx))[ab]
        if c == 0:
            gains[ab].wait()
        loads[c, 2 * ab].wait()
        loads[c, 2 * ab + 1].wait()
        for p in range(PLANE):
            pair = c * PLANE + p
            t = (raw[:, cols(pair)].astype(F32) * gain[pair:pair + 1, :]).astype(BF16)
            mult[:, cols(pair)] = t
            own[c, ab, p] = fold(dot(t, other[:, cols(pair)], 0, 0))

    units = [(c, ab) for c in range(CHUNKS) for ab in range(2)]
    for c, ab in units:
        own_state(c, ab)
        if (c, ab) == (0, 0):
            count = len(hops) + len(dp_bits)
            for d in dists:
                count = count + (z + d < nz).astype(jnp.int32) + (z >= d).astype(jnp.int32)
            pl.semaphore_wait(barrier, count)
        for h in (2, 0, 1):
            copy1(c, ab, h).start()
        rx1[c, ab, slot] = own[c, ab, slot]

    row = lax.broadcasted_iota(jnp.int32, (rows, 2 * rows), 0)
    col = lax.broadcasted_iota(jnp.int32, (rows, 2 * rows), 1) % rows
    low = row >= col
    high = col >= row

    def intra(pair):
        sl = cols(pair)
        gv, vv, qv, kv = gx[:, sl], vx[:, sl], gq[:, sl], gk[:, sl]
        gs, qs = stack(gv), stack(qv)
        pg = jnp.where(low, dot(gv, stack(vv), 1, 1), 0.0).astype(BF16)
        dq = score_scale * dot(pg, stack(kv), 1, 0)
        dqs[:, sl] = dq
        gtx[0, 0, pair:pair + 1, :] = jnp.sum(dq * qx[:, sl].astype(F32), axis=0, keepdims=True)
        pgt = jnp.where(high, dot(vv, gs, 1, 1), 0.0).astype(BF16)
        dk = score_scale * dot(pgt, qs, 1, 0)
        dks[:, sl] = dk
        gtx[0, 1, pair:pair + 1, :] = jnp.sum(dk * kx[:, sl].astype(F32), axis=0, keepdims=True)
        pst = jnp.where(high, dot(kv, qs, 1, 1), 0.0).astype(BF16)
        dvs[:, sl] = score_scale * dot(pst, gs, 1, 0)

    steps = len(dists)

    def totals(c, ab):
        for h in range(3):
            copy1(c, ab, h).wait_recv()
        zs[0, c, ab] = (rx1[c, ab, 0] + rx1[c, ab, 1]) + (rx1[c, ab, 2] + rx1[c, ab, 3])
        exc[c, ab] = jnp.zeros_like(exc[c, ab])
        if dists:
            @pl.when(sends(0, ab))
            def _():
                copyz(c, 0, ab).start()

    def scan(s, c, ab):
        @pl.when(takes(s, ab))
        def _():
            copyz(c, s, ab).wait_recv()
            got = zr[s, c, ab]
            exc[c, ab] = exc[c, ab] + got
            if s + 1 < steps:
                zs[s + 1, c, ab] = zs[s, c, ab] + got
        if s + 1 < steps:
            @pl.when(jnp.logical_not(takes(s, ab)))
            def _():
                zs[s + 1, c, ab] = zs[s, c, ab]

            @pl.when(sends(s + 1, ab))
            def _():
                copyz(c, s + 1, ab).start()

    def give(c, ab):
        run = exc[c, ab]
        order = list(range(PLANE)) if ab == 0 else list(reversed(range(PLANE)))
        for p in order:
            tx2[c, ab, p] = run
            if p != order[-1]:
                run = run + rx1[c, ab, p]
        for h in (2, 0, 1):
            copy2(c, ab, h).start()
        rx2[c, ab, slot] = tx2[c, ab, slot]
        if ab == 0:
            return
        both = tx2[c, 0, 0] * rx1[c, 1, 0]
        for p in range(1, PLANE):
            both = both + tx2[c, 0, p] * rx1[c, 1, p]
        spread = jnp.concatenate([jnp.where(left, both, 0.0), jnp.where(left, 0.0, both)], axis=0)
        line = lax.dot_general(
            jnp.ones((8, LANES), F32), spread, (((1,), (1,)), ((), ())),
            precision=lax.Precision.HIGHEST, preferred_element_type=F32)
        gtx[0, 2, pl.ds(c * PLANE + slot, 1), :] = line[:1] * score_scale

    def final(c):
        for ab in range(2):
            for h in range(3):
                copy2(c, ab, h).wait_recv()
        for p in range(PLANE):
            pair = c * PLANE + p
            sl = cols(pair)
            sa = stack(rx2[c, 0, p].astype(BF16))
            sb = stack(rx2[c, 1, p].astype(BF16))
            dq = dqs[:, sl] + score_scale * dot(gx[:, sl], sa, 1, 1)
            dk = dks[:, sl] + score_scale * dot(vx[:, sl], sb, 1, 1)
            dv = dvs[:, sl] + score_scale * dot(gk[:, sl], sb, 1, 0)
            qo[0, :, sl] = (dq * gain_q[pair:pair + 1, :]).astype(BF16)
            ko[0, :, sl] = (dk * gain_k[pair:pair + 1, :]).astype(BF16)
            vo[0, :, sl] = dv.astype(BF16)

    gtx[0, 2] = jnp.zeros((PAIRS, LANES), F32)
    for pair in range(PAIRS):
        intra(pair)
    for turn in range(len(units) + steps):
        for stage in range(steps + 1):
            if 0 <= turn - stage < len(units):
                c, ab = units[turn - stage]
                if stage == 0:
                    totals(c, ab)
                else:
                    scan(stage - 1, c, ab)
                if stage == steps:
                    give(c, ab)

    partners = [{"dp": dp + d * (1 - 2 * ((dp // d) % 2))} for d in dp_bits]
    for d in [d * PLANE for d in dists]:
        partners.append({"seq": me + d * (1 - 2 * ((me // d) % 2))})

    def copyg(i):
        return pltpu.make_async_remote_copy(
            src_ref=gtx.at[i], dst_ref=grx.at[i], send_sem=sg.at[i], recv_sem=rg.at[i],
            device_id=partners[i], device_id_type=MESH)

    def copyp(h):
        return pltpu.make_async_remote_copy(
            src_ref=gtx.at[last], dst_ref=gpl.at[slot], send_sem=sp.at[h], recv_sem=rp.at[h],
            device_id={"seq": me + hops[h]}, device_id_type=MESH)

    last = len(partners)
    for i in range(last):
        copyg(i).start()
        copyg(i).wait_recv()
        gtx[i + 1] = gtx[i] + grx[i]
    for h in (2, 0, 1):
        copyp(h).start()
    gpl[slot] = gtx[last]
    for c in range(CHUNKS):
        final(c)
    for h in range(3):
        copyp(h).wait_recv()
    total = (gpl[0] + gpl[1]) + (gpl[2] + gpl[3])
    gqo[...] = (total[0] + total[2] / gain_q[...]) * factor
    gko[...] = (total[1] + total[2] / gain_k[...]) * factor

    for c in range(CHUNKS):
        for ab in range(2):
            for h in range(3):
                copy1(c, ab, h).wait_send()
                copy2(c, ab, h).wait_send()
        for s in range(len(dists)):
            for ab in range(2):
                @pl.when(sends(s, ab))
                def _():
                    copyz(c, s, ab).wait_send()
    for i in range(last):
        copyg(i).wait_send()
    for h in range(3):
        copyp(h).wait_send()


def move(*refs):
    sem = refs[-1]
    half = (len(refs) - 1) // 2
    copies = [pltpu.make_async_copy(refs[i], refs[half + i], sem.at[i]) for i in range(half)]
    for cp in copies:
        cp.start()
    for cp in copies:
        cp.wait()


def solution(mesh):
    n = mesh.shape["seq"]
    ndp = mesh.shape["dp"]
    steps = max(1, (n // PLANE - 1).bit_length())
    gsteps = max(1, (n // PLANE - 1).bit_length() + (ndp - 1).bit_length())

    def local(query_rows, key_rows, value_rows, out_grad, query_gain, key_gain):
        rows, width = query_rows.shape[1:]
        seq_len = rows * n
        score_scale = 1.0 / math.sqrt(HEAD_DIM * seq_len)
        factor = 1.0 / math.sqrt(seq_len * ndp)
        big = jax.ShapeDtypeStruct(query_rows.shape, BF16)
        small = jax.ShapeDtypeStruct((PAIRS, LANES), F32)
        hbm = pl.BlockSpec(memory_space=pltpu.HBM)
        unit = (HEAD_DIM, LANES)
        dma = pltpu.SemaphoreType.DMA
        out = pl.pallas_call(
            functools.partial(kernel, n, ndp, rows, score_scale, factor),
            out_shape=[big, big, big, small, small],
            in_specs=[hbm] * 6,
            out_specs=[pl.BlockSpec(memory_space=pltpu.VMEM)] * 5,
            scratch_shapes=[pltpu.VMEM((rows, width), BF16)] * 6
            + [pltpu.VMEM((PAIRS, LANES), F32)] * 2
            + [pltpu.VMEM((rows, width), F32)] * 3
            + [
                pltpu.VMEM((CHUNKS, 2, PLANE) + unit, F32),
                pltpu.VMEM((CHUNKS, 2, PLANE) + unit, F32),
                pltpu.VMEM((steps, CHUNKS, 2) + unit, F32),
                pltpu.VMEM((steps, CHUNKS, 2) + unit, F32),
                pltpu.VMEM((CHUNKS, 2) + unit, F32),
                pltpu.VMEM((CHUNKS, 2, PLANE) + unit, F32),
                pltpu.VMEM((CHUNKS, 2, PLANE) + unit, F32),
                pltpu.VMEM((gsteps + 1, 3, PAIRS, LANES), F32),
                pltpu.VMEM((gsteps, 3, PAIRS, LANES), F32),
                pltpu.VMEM((PLANE, 3, PAIRS, LANES), F32),
                dma((CHUNKS, 4)), dma((2,)),
                dma((CHUNKS, 2, 3)), dma((CHUNKS, 2, 3)),
                dma((steps, CHUNKS, 2)), dma((steps, CHUNKS, 2)),
                dma((CHUNKS, 2, 3)), dma((CHUNKS, 2, 3)),
                dma((gsteps,)), dma((gsteps,)), dma((3,)), dma((3,)),
            ],
            compiler_params=pltpu.CompilerParams(
                collective_id=0, has_side_effects=True, vmem_limit_bytes=32 * 1024 * 1024
            ),
        )(*[pltpu.with_memory_space_constraint(t, pltpu.HBM) for t in (
            query_rows, key_rows, value_rows, out_grad,
            query_gain.reshape(PAIRS, LANES), key_gain.reshape(PAIRS, LANES))])
        out = pl.pallas_call(
            move,
            out_shape=[big, big, big, small, small],
            in_specs=[pl.BlockSpec(memory_space=pltpu.VMEM)] * 5,
            out_specs=[hbm] * 5,
            scratch_shapes=[dma((5,))],
        )(*[pltpu.with_memory_space_constraint(t, pltpu.VMEM) for t in out])
        return (out[0], out[1], out[2], out[3].reshape(width), out[4].reshape(width))

    spec = P("dp", "seq", None)
    return jax.shard_map(local, mesh=mesh, in_specs=(spec,) * 4 + (P(), P()),
                         out_specs=(spec, spec, spec, P(), P()), check_vma=False)
```

```python
import functools
import math

import jax
import jax.numpy as jnp
from jax import lax
from jax.experimental import pallas as pl
from jax.experimental.pallas import tpu as pltpu
from jax.sharding import PartitionSpec as P

HEADS = 16
HEAD_DIM = 64
PLANE = 4
MESH = pl.DeviceIdType.MESH
F32 = jnp.float32
BF16 = jnp.bfloat16
LANES = 2 * HEAD_DIM
PAIRS = HEADS // 2
CHUNKS = PAIRS // PLANE
AHEAD = 3
HOLD = 2


def dot(a, b, da, db):
    return lax.dot_general(a, b, (((da,), (db,)), ((), ())), preferred_element_type=F32)


def kernel(n, ndp, rows, score_scale, factor, q_h, k_h, v_h, g_h, gq_h, gk_h,
           qo, ko, vo, gqo, gko,
           qx, kx, vx, gx, gq, gk, gain_q, gain_k, dqs, dks, dvs,
           own, rx1, zs, zr, exc, tx2, rx2, gtx, grx, gpl,
           in_sem, gain_sem, s1, r1, sz, rz, s2, r2, sg, rg, sp, rp):
    nz = n // PLANE
    dists = list(range(1, nz))
    z_bits = [d for d in dists if d & (d - 1) == 0]
    me = lax.axis_index("seq")
    dp = lax.axis_index("dp")
    z = me // PLANE
    slot = me % PLANE
    x = slot % 2
    y = slot // 2
    fx = 1 - 2 * x
    fy = 2 - 4 * y
    hops = [fx, fy, fx + fy]

    barrier = pltpu.get_barrier_semaphore()

    def greet(**where):
        pl.semaphore_signal(barrier, inc=1, device_id=where, device_id_type=MESH)

    for h in hops:
        greet(seq=me + h)
    for d in dists:
        @pl.when(z + d < nz)
        def _(d=d):
            greet(seq=me + d * PLANE)

        @pl.when(z >= d)
        def _(d=d):
            greet(seq=me - d * PLANE)
    dp_bits = []
    d = 1
    while d < ndp:
        dp_bits.append(d)
        d *= 2
    for d in dp_bits:
        greet(dp=dp + d * (1 - 2 * ((dp // d) % 2)))

    span = PLANE * LANES

    def part(c):
        return pl.ds(c * span, span)

    gains = []
    for i, (src, dst) in enumerate(((gk_h, gain_k), (gq_h, gain_q))):
        gains.append(pltpu.make_async_copy(src, dst, gain_sem.at[i]))
        gains[i].start()
    loads = {}
    for c in range(CHUNKS):
        for i, (src, dst) in enumerate(((k_h, kx), (v_h, vx), (q_h, qx), (g_h, gx))):
            loads[c, i] = pltpu.make_async_copy(
                src.at[0, :, part(c)], dst.at[:, part(c)], in_sem.at[c, i])
            loads[c, i].start()

    lane = lax.broadcasted_iota(jnp.int32, (1, LANES), 1)
    first = (lane < HEAD_DIM).astype(F32).astype(BF16)
    second = (lane >= HEAD_DIM).astype(F32).astype(BF16)
    left = lax.broadcasted_iota(jnp.int32, (HEAD_DIM, LANES), 1) < HEAD_DIM

    def stack(t):
        return jnp.concatenate([t * first, t * second], axis=0)

    def cols(pair):
        return pl.ds(pair * LANES, LANES)

    def fold(full):
        return jnp.where(left, full[:HEAD_DIM], full[HEAD_DIM:])

    def copy1(c, ab, h):
        hop = hops[h]
        return pltpu.make_async_remote_copy(
            src_ref=own.at[c, ab, slot + hop], dst_ref=rx1.at[c, ab, slot],
            send_sem=s1.at[c, ab, h], recv_sem=r1.at[c, ab, h],
            device_id={"seq": me + hop}, device_id_type=MESH)

    def copy2(c, ab, h):
        hop = hops[h]
        return pltpu.make_async_remote_copy(
            src_ref=tx2.at[c, ab, slot + hop], dst_ref=rx2.at[c, ab, slot],
            send_sem=s2.at[c, ab, h], recv_sem=r2.at[c, ab, h],
            device_id={"seq": me + hop}, device_id_type=MESH)

    def copyz(c, s, ab):
        to = me + dists[s] * PLANE if ab == 0 else me - dists[s] * PLANE
        return pltpu.make_async_remote_copy(
            src_ref=zs.at[0, c, ab], dst_ref=zr.at[s, c, ab],
            send_sem=sz.at[s, c, ab], recv_sem=rz.at[s, c, ab],
            device_id={"seq": to}, device_id_type=MESH)

    def sends(s, ab):
        return z + dists[s] < nz if ab == 0 else z >= dists[s]

    def takes(s, ab):
        return z >= dists[s] if ab == 0 else z + dists[s] < nz

    def own_state(c, ab):
        raw, gain, mult, other = ((kx, gain_k, gk, vx), (qx, gain_q, gq, gx))[ab]
        if c == 0:
            gains[ab].wait()
        loads[c, 2 * ab].wait()
        loads[c, 2 * ab + 1].wait()
        for p in range(PLANE):
            pair = c * PLANE + p
            t = (raw[:, cols(pair)].astype(F32) * gain[pair:pair + 1, :]).astype(BF16)
            mult[:, cols(pair)] = t
            own[c, ab, p] = fold(dot(t, other[:, cols(pair)], 0, 0))

    units = [(c, ab) for c in range(CHUNKS) for ab in range(2)]

    def send(c, ab):
        own_state(c, ab)
        if (c, ab) == (0, 0):
            count = len(hops) + len(dp_bits)
            for d in dists:
                count = count + (z + d < nz).astype(jnp.int32) + (z >= d).astype(jnp.int32)
            pl.semaphore_wait(barrier, count)
        for h in (2, 0, 1):
            copy1(c, ab, h).start()
        rx1[c, ab, slot] = own[c, ab, slot]

    for u in units[:AHEAD]:
        send(*u)

    row = lax.broadcasted_iota(jnp.int32, (rows, 2 * rows), 0)
    col = lax.broadcasted_iota(jnp.int32, (rows, 2 * rows), 1) % rows
    low = row >= col
    high = col >= row

    def intra(pair):
        sl = cols(pair)
        gv, vv, qv, kv = gx[:, sl], vx[:, sl], gq[:, sl], gk[:, sl]
        gs, qs = stack(gv), stack(qv)
        pg = jnp.where(low, dot(gv, stack(vv), 1, 1), 0.0).astype(BF16)
        dq = score_scale * dot(pg, stack(kv), 1, 0)
        dqs[:, sl] = dq
        gtx[0, 0, pair:pair + 1, :] = jnp.sum(dq * qx[:, sl].astype(F32), axis=0, keepdims=True)
        pgt = jnp.where(high, dot(vv, gs, 1, 1), 0.0).astype(BF16)
        dk = score_scale * dot(pgt, qs, 1, 0)
        dks[:, sl] = dk
        gtx[0, 1, pair:pair + 1, :] = jnp.sum(dk * kx[:, sl].astype(F32), axis=0, keepdims=True)
        pst = jnp.where(high, dot(kv, qs, 1, 1), 0.0).astype(BF16)
        dvs[:, sl] = score_scale * dot(pst, gs, 1, 0)


    def totals(c, ab):
        for h in range(3):
            copy1(c, ab, h).wait_recv()
        zs[0, c, ab] = (rx1[c, ab, 0] + rx1[c, ab, 1]) + (rx1[c, ab, 2] + rx1[c, ab, 3])
        exc[c, ab] = jnp.zeros_like(exc[c, ab])
        for s in range(len(dists)):
            @pl.when(sends(s, ab))
            def _():
                copyz(c, s, ab).start()

    def scan(c, ab):
        for s in range(len(dists)):
            @pl.when(takes(s, ab))
            def _():
                copyz(c, s, ab).wait_recv()
                exc[c, ab] = exc[c, ab] + zr[s, c, ab]

    def give(c, ab):
        run = exc[c, ab]
        order = list(range(PLANE)) if ab == 0 else list(reversed(range(PLANE)))
        for p in order:
            tx2[c, ab, p] = run
            if p != order[-1]:
                run = run + rx1[c, ab, p]
        if ab == 0:
            both = tx2[c, 0, 0] * rx1[c, 1, 0]
            for p in range(1, PLANE):
                both = both + tx2[c, 0, p] * rx1[c, 1, p]
            spread = jnp.concatenate(
                [jnp.where(left, both, 0.0), jnp.where(left, 0.0, both)], axis=0)
            line = lax.dot_general(
                jnp.ones((8, LANES), F32), spread, (((1,), (1,)), ((), ())),
                precision=lax.Precision.HIGHEST, preferred_element_type=F32)
            gtx[0, 2, pl.ds(c * PLANE + slot, 1), :] = line[:1] * score_scale
            if c == CHUNKS - 1 and last:
                copyg(0).start()
        for h in (2, 0, 1):
            copy2(c, ab, h).start()
        rx2[c, ab, slot] = tx2[c, ab, slot]

    def final(c):
        for ab in range(2):
            for h in range(3):
                copy2(c, ab, h).wait_recv()
        for p in range(PLANE):
            pair = c * PLANE + p
            sl = cols(pair)
            sa = stack(rx2[c, 0, p].astype(BF16))
            sb = stack(rx2[c, 1, p].astype(BF16))
            dq = dqs[:, sl] + score_scale * dot(gx[:, sl], sa, 1, 1)
            dk = dks[:, sl] + score_scale * dot(vx[:, sl], sb, 1, 1)
            dv = dvs[:, sl] + score_scale * dot(gk[:, sl], sb, 1, 0)
            qo[0, :, sl] = (dq * gain_q[pair:pair + 1, :]).astype(BF16)
            ko[0, :, sl] = (dk * gain_k[pair:pair + 1, :]).astype(BF16)
            vo[0, :, sl] = dv.astype(BF16)

    gtx[0, 2] = jnp.zeros((PAIRS, LANES), F32)
    partners = [{"dp": dp + d * (1 - 2 * ((dp // d) % 2))} for d in dp_bits]
    for d in [d * PLANE for d in z_bits]:
        partners.append({"seq": me + d * (1 - 2 * ((me // d) % 2))})

    def copyg(i):
        return pltpu.make_async_remote_copy(
            src_ref=gtx.at[i], dst_ref=grx.at[i], send_sem=sg.at[i], recv_sem=rg.at[i],
            device_id=partners[i], device_id_type=MESH)

    def copyp(h):
        return pltpu.make_async_remote_copy(
            src_ref=gtx.at[last], dst_ref=gpl.at[slot], send_sem=sp.at[h], recv_sem=rp.at[h],
            device_id={"seq": me + hops[h]}, device_id_type=MESH)

    last = len(partners)
    left_over = list(range(PAIRS))
    for turn in range(len(units) + HOLD):
        if turn < len(units):
            totals(*units[turn])
            if turn + AHEAD < len(units):
                send(*units[turn + AHEAD])
            if turn + AHEAD + 1 >= len(units):
                while left_over:
                    intra(left_over.pop(0))
        if turn >= HOLD:
            scan(*units[turn - HOLD])
            give(*units[turn - HOLD])

    for i in range(last):
        if i > 0:
            copyg(i).start()
        copyg(i).wait_recv()
        gtx[i + 1] = gtx[i] + grx[i]
    for h in (2, 0, 1):
        copyp(h).start()
    gpl[slot] = gtx[last]
    for c in range(CHUNKS):
        final(c)
    for h in range(3):
        copyp(h).wait_recv()
    total = (gpl[0] + gpl[1]) + (gpl[2] + gpl[3])
    gqo[...] = (total[0] + total[2] / gain_q[...]) * factor
    gko[...] = (total[1] + total[2] / gain_k[...]) * factor

    for c in range(CHUNKS):
        for ab in range(2):
            for h in range(3):
                copy1(c, ab, h).wait_send()
                copy2(c, ab, h).wait_send()
        for s in range(len(dists)):
            for ab in range(2):
                @pl.when(sends(s, ab))
                def _():
                    copyz(c, s, ab).wait_send()
    for i in range(last):
        copyg(i).wait_send()
    for h in range(3):
        copyp(h).wait_send()


def move(*refs):
    sem = refs[-1]
    half = (len(refs) - 1) // 2
    copies = [pltpu.make_async_copy(refs[i], refs[half + i], sem.at[i]) for i in range(half)]
    for cp in copies:
        cp.start()
    for cp in copies:
        cp.wait()


def solution(mesh):
    n = mesh.shape["seq"]
    ndp = mesh.shape["dp"]
    steps = max(1, n // PLANE - 1)
    gsteps = max(1, (n // PLANE - 1).bit_length() + (ndp - 1).bit_length())

    def local(query_rows, key_rows, value_rows, out_grad, query_gain, key_gain):
        rows, width = query_rows.shape[1:]
        seq_len = rows * n
        score_scale = 1.0 / math.sqrt(HEAD_DIM * seq_len)
        factor = 1.0 / math.sqrt(seq_len * ndp)
        big = jax.ShapeDtypeStruct(query_rows.shape, BF16)
        small = jax.ShapeDtypeStruct((PAIRS, LANES), F32)
        hbm = pl.BlockSpec(memory_space=pltpu.HBM)
        unit = (HEAD_DIM, LANES)
        dma = pltpu.SemaphoreType.DMA
        out = pl.pallas_call(
            functools.partial(kernel, n, ndp, rows, score_scale, factor),
            out_shape=[big, big, big, small, small],
            in_specs=[hbm] * 6,
            out_specs=[pl.BlockSpec(memory_space=pltpu.VMEM)] * 5,
            scratch_shapes=[pltpu.VMEM((rows, width), BF16)] * 6
            + [pltpu.VMEM((PAIRS, LANES), F32)] * 2
            + [pltpu.VMEM((rows, width), F32)] * 3
            + [
                pltpu.VMEM((CHUNKS, 2, PLANE) + unit, F32),
                pltpu.VMEM((CHUNKS, 2, PLANE) + unit, F32),
                pltpu.VMEM((1, CHUNKS, 2) + unit, F32),
                pltpu.VMEM((steps, CHUNKS, 2) + unit, F32),
                pltpu.VMEM((CHUNKS, 2) + unit, F32),
                pltpu.VMEM((CHUNKS, 2, PLANE) + unit, F32),
                pltpu.VMEM((CHUNKS, 2, PLANE) + unit, F32),
                pltpu.VMEM((gsteps + 1, 3, PAIRS, LANES), F32),
                pltpu.VMEM((gsteps, 3, PAIRS, LANES), F32),
                pltpu.VMEM((PLANE, 3, PAIRS, LANES), F32),
                dma((CHUNKS, 4)), dma((2,)),
                dma((CHUNKS, 2, 3)), dma((CHUNKS, 2, 3)),
                dma((steps, CHUNKS, 2)), dma((steps, CHUNKS, 2)),
                dma((CHUNKS, 2, 3)), dma((CHUNKS, 2, 3)),
                dma((gsteps,)), dma((gsteps,)), dma((3,)), dma((3,)),
            ],
            compiler_params=pltpu.CompilerParams(
                collective_id=0, has_side_effects=True, vmem_limit_bytes=32 * 1024 * 1024
            ),
        )(*[pltpu.with_memory_space_constraint(t, pltpu.HBM) for t in (
            query_rows, key_rows, value_rows, out_grad,
            query_gain.reshape(PAIRS, LANES), key_gain.reshape(PAIRS, LANES))])
        out = pl.pallas_call(
            move,
            out_shape=[big, big, big, small, small],
            in_specs=[pl.BlockSpec(memory_space=pltpu.VMEM)] * 5,
            out_specs=[hbm] * 5,
            scratch_shapes=[dma((5,))],
        )(*[pltpu.with_memory_space_constraint(t, pltpu.VMEM) for t in out])
        return (out[0], out[1], out[2], out[3].reshape(width), out[4].reshape(width))

    spec = P("dp", "seq", None)
    return jax.shard_map(local, mesh=mesh, in_specs=(spec,) * 4 + (P(), P()),
                         out_specs=(spec, spec, spec, P(), P()), check_vma=False)
```

```python
import functools
import math

import jax
import jax.numpy as jnp
from jax import lax
from jax.experimental import pallas as pl
from jax.experimental.pallas import tpu as pltpu
from jax.sharding import PartitionSpec as P

HEADS = 16
HEAD_DIM = 64
PLANE = 4
MESH = pl.DeviceIdType.MESH
F32 = jnp.float32
BF16 = jnp.bfloat16
LANES = 2 * HEAD_DIM
PAIRS = HEADS // 2
CHUNKS = PAIRS // PLANE
AHEAD = 3
HOLD = 2


def dot(a, b, da, db):
    return lax.dot_general(a, b, (((da,), (db,)), ((), ())), preferred_element_type=F32)


def kernel(n, ndp, rows, score_scale, factor, q_h, k_h, v_h, g_h, gq_h, gk_h,
           qo, ko, vo, gqo, gko,
           qx, kx, vx, gx, gq, gk, gain_q, gain_k, dqs, dks, dvs,
           own, rx1, zs, zr, exc, tx2, rx2, gtx, grx, gpl,
           in_sem, gain_sem, s1, r1, sz, rz, s2, r2, sg, rg, sp, rp):
    nz = n // PLANE
    dists = list(range(1, nz))
    z_bits = [d for d in dists if d & (d - 1) == 0]
    me = lax.axis_index("seq")
    dp = lax.axis_index("dp")
    z = me // PLANE
    slot = me % PLANE
    x = slot % 2
    y = slot // 2
    fx = 1 - 2 * x
    fy = 2 - 4 * y
    hops = [fx, fy, fx + fy]

    barrier = pltpu.get_barrier_semaphore()

    def greet(**where):
        pl.semaphore_signal(barrier, inc=1, device_id=where, device_id_type=MESH)

    for h in hops:
        greet(seq=me + h)
    for d in dists:
        @pl.when(z + d < nz)
        def _(d=d):
            greet(seq=me + d * PLANE)

        @pl.when(z >= d)
        def _(d=d):
            greet(seq=me - d * PLANE)
    dp_bits = []
    d = 1
    while d < ndp:
        dp_bits.append(d)
        d *= 2
    for d in dp_bits:
        greet(dp=dp + d * (1 - 2 * ((dp // d) % 2)))

    span = PLANE * LANES

    def part(c):
        return pl.ds(c * span, span)

    gains = []
    for i, (src, dst) in enumerate(((gk_h, gain_k), (gq_h, gain_q))):
        gains.append(pltpu.make_async_copy(src, dst, gain_sem.at[i]))
        gains[i].start()
    loads = {}
    for c in range(CHUNKS):
        for i, (src, dst) in enumerate(((k_h, kx), (v_h, vx), (q_h, qx), (g_h, gx))):
            loads[c, i] = pltpu.make_async_copy(
                src.at[0, :, part(c)], dst.at[:, part(c)], in_sem.at[c, i])
            loads[c, i].start()

    lane = lax.broadcasted_iota(jnp.int32, (1, LANES), 1)
    first = (lane < HEAD_DIM).astype(F32).astype(BF16)
    second = (lane >= HEAD_DIM).astype(F32).astype(BF16)
    left = lax.broadcasted_iota(jnp.int32, (HEAD_DIM, LANES), 1) < HEAD_DIM

    def stack(t):
        return jnp.concatenate([t * first, t * second], axis=0)

    def cols(pair):
        return pl.ds(pair * LANES, LANES)

    def fold(full):
        return jnp.where(left, full[:HEAD_DIM], full[HEAD_DIM:])

    def copy1(c, ab, h):
        hop = hops[h]
        return pltpu.make_async_remote_copy(
            src_ref=own.at[c, ab, slot + hop], dst_ref=rx1.at[c, ab, slot],
            send_sem=s1.at[c, ab, h], recv_sem=r1.at[c, ab, h],
            device_id={"seq": me + hop}, device_id_type=MESH)

    def copy2(c, ab, h):
        hop = hops[h]
        return pltpu.make_async_remote_copy(
            src_ref=tx2.at[c, ab, slot + hop], dst_ref=rx2.at[c, ab, slot],
            send_sem=s2.at[c, ab, h], recv_sem=r2.at[c, ab, h],
            device_id={"seq": me + hop}, device_id_type=MESH)

    def copyz(c, s, ab):
        to = me + dists[s] * PLANE if ab == 0 else me - dists[s] * PLANE
        return pltpu.make_async_remote_copy(
            src_ref=zs.at[0, c, ab], dst_ref=zr.at[s, c, ab],
            send_sem=sz.at[s, c, ab], recv_sem=rz.at[s, c, ab],
            device_id={"seq": to}, device_id_type=MESH)

    def sends(s, ab):
        return z + dists[s] < nz if ab == 0 else z >= dists[s]

    def takes(s, ab):
        return z >= dists[s] if ab == 0 else z + dists[s] < nz

    def own_state(c, ab):
        raw, gain, mult, other = ((kx, gain_k, gk, vx), (qx, gain_q, gq, gx))[ab]
        if c == 0:
            gains[ab].wait()
        loads[c, 2 * ab].wait()
        loads[c, 2 * ab + 1].wait()
        for p in range(PLANE):
            pair = c * PLANE + p
            t = (raw[:, cols(pair)].astype(F32) * gain[pair:pair + 1, :]).astype(BF16)
            mult[:, cols(pair)] = t
            own[c, ab, p] = fold(dot(t, other[:, cols(pair)], 0, 0))

    units = [(c, ab) for c in range(CHUNKS) for ab in range(2)]

    def send(c, ab):
        own_state(c, ab)
        if (c, ab) == (0, 0):
            count = len(hops) + len(dp_bits)
            for d in dists:
                count = count + (z + d < nz).astype(jnp.int32) + (z >= d).astype(jnp.int32)
            pl.semaphore_wait(barrier, count)
        for h in (2, 0, 1):
            copy1(c, ab, h).start()
        rx1[c, ab, slot] = own[c, ab, slot]

    for u in units[:AHEAD]:
        send(*u)

    row = lax.broadcasted_iota(jnp.int32, (rows, 2 * rows), 0)
    col = lax.broadcasted_iota(jnp.int32, (rows, 2 * rows), 1) % rows
    low = row >= col
    high = col >= row

    def intra(pair):
        sl = cols(pair)
        gv, vv, qv, kv = gx[:, sl], vx[:, sl], gq[:, sl], gk[:, sl]
        gs, qs = stack(gv), stack(qv)
        pg = jnp.where(low, dot(gv, stack(vv), 1, 1), 0.0).astype(BF16)
        dq = score_scale * dot(pg, stack(kv), 1, 0)
        dqs[:, sl] = dq
        gtx[0, 0, pair:pair + 1, :] = jnp.sum(dq * qx[:, sl].astype(F32), axis=0, keepdims=True)
        pgt = jnp.where(high, dot(vv, gs, 1, 1), 0.0).astype(BF16)
        dk = score_scale * dot(pgt, qs, 1, 0)
        dks[:, sl] = dk
        gtx[0, 1, pair:pair + 1, :] = jnp.sum(dk * kx[:, sl].astype(F32), axis=0, keepdims=True)
        pst = jnp.where(high, dot(kv, qs, 1, 1), 0.0).astype(BF16)
        dvs[:, sl] = score_scale * dot(pst, gs, 1, 0)


    def totals(c, ab):
        for h in range(3):
            copy1(c, ab, h).wait_recv()
        zs[0, c, ab] = (rx1[c, ab, 0] + rx1[c, ab, 1]) + (rx1[c, ab, 2] + rx1[c, ab, 3])
        exc[c, ab] = jnp.zeros_like(exc[c, ab])
        for s in reversed(range(len(dists))):
            @pl.when(sends(s, ab))
            def _():
                copyz(c, s, ab).start()

    def scan(c, ab):
        for s in range(len(dists)):
            @pl.when(takes(s, ab))
            def _():
                copyz(c, s, ab).wait_recv()
                exc[c, ab] = exc[c, ab] + zr[s, c, ab]

    def give(c, ab):
        run = exc[c, ab]
        order = list(range(PLANE)) if ab == 0 else list(reversed(range(PLANE)))
        for p in order:
            tx2[c, ab, p] = run
            if p != order[-1]:
                run = run + rx1[c, ab, p]
        if ab == 0:
            both = tx2[c, 0, 0] * rx1[c, 1, 0]
            for p in range(1, PLANE):
                both = both + tx2[c, 0, p] * rx1[c, 1, p]
            spread = jnp.concatenate(
                [jnp.where(left, both, 0.0), jnp.where(left, 0.0, both)], axis=0)
            line = lax.dot_general(
                jnp.ones((8, LANES), F32), spread, (((1,), (1,)), ((), ())),
                precision=lax.Precision.HIGHEST, preferred_element_type=F32)
            gtx[0, 2, pl.ds(c * PLANE + slot, 1), :] = line[:1] * score_scale
            if c == CHUNKS - 1 and last:
                copyg(0).start()
        for h in (2, 0, 1):
            copy2(c, ab, h).start()
        rx2[c, ab, slot] = tx2[c, ab, slot]

    def final(c):
        for ab in range(2):
            for h in range(3):
                copy2(c, ab, h).wait_recv()
        for p in range(PLANE):
            pair = c * PLANE + p
            sl = cols(pair)
            sa = stack(rx2[c, 0, p].astype(BF16))
            sb = stack(rx2[c, 1, p].astype(BF16))
            dq = dqs[:, sl] + score_scale * dot(gx[:, sl], sa, 1, 1)
            dk = dks[:, sl] + score_scale * dot(vx[:, sl], sb, 1, 1)
            dv = dvs[:, sl] + score_scale * dot(gk[:, sl], sb, 1, 0)
            qo[0, :, sl] = (dq * gain_q[pair:pair + 1, :]).astype(BF16)
            ko[0, :, sl] = (dk * gain_k[pair:pair + 1, :]).astype(BF16)
            vo[0, :, sl] = dv.astype(BF16)

    gtx[0, 2] = jnp.zeros((PAIRS, LANES), F32)
    partners = [{"dp": dp + d * (1 - 2 * ((dp // d) % 2))} for d in dp_bits]
    for d in [d * PLANE for d in z_bits]:
        partners.append({"seq": me + d * (1 - 2 * ((me // d) % 2))})

    def copyg(i):
        return pltpu.make_async_remote_copy(
            src_ref=gtx.at[i], dst_ref=grx.at[i], send_sem=sg.at[i], recv_sem=rg.at[i],
            device_id=partners[i], device_id_type=MESH)

    def copyp(h):
        return pltpu.make_async_remote_copy(
            src_ref=gtx.at[last], dst_ref=gpl.at[slot], send_sem=sp.at[h], recv_sem=rp.at[h],
            device_id={"seq": me + hops[h]}, device_id_type=MESH)

    last = len(partners)
    left_over = list(range(PAIRS))
    for turn in range(len(units) + HOLD):
        if turn < len(units):
            totals(*units[turn])
            if turn + AHEAD < len(units):
                send(*units[turn + AHEAD])
            if turn + AHEAD + 1 >= len(units):
                while left_over:
                    intra(left_over.pop(0))
        if turn >= HOLD:
            scan(*units[turn - HOLD])
            give(*units[turn - HOLD])

    for i in range(last):
        if i > 0:
            copyg(i).start()
        copyg(i).wait_recv()
        gtx[i + 1] = gtx[i] + grx[i]
    for h in (2, 0, 1):
        copyp(h).start()
    gpl[slot] = gtx[last]
    for c in range(CHUNKS):
        final(c)
    for h in range(3):
        copyp(h).wait_recv()
    total = (gpl[0] + gpl[1]) + (gpl[2] + gpl[3])
    gqo[...] = (total[0] + total[2] / gain_q[...]) * factor
    gko[...] = (total[1] + total[2] / gain_k[...]) * factor

    for c in range(CHUNKS):
        for ab in range(2):
            for h in range(3):
                copy1(c, ab, h).wait_send()
                copy2(c, ab, h).wait_send()
        for s in range(len(dists)):
            for ab in range(2):
                @pl.when(sends(s, ab))
                def _():
                    copyz(c, s, ab).wait_send()
    for i in range(last):
        copyg(i).wait_send()
    for h in range(3):
        copyp(h).wait_send()


def move(*refs):
    sem = refs[-1]
    half = (len(refs) - 1) // 2
    copies = [pltpu.make_async_copy(refs[i], refs[half + i], sem.at[i]) for i in range(half)]
    for cp in copies:
        cp.start()
    for cp in copies:
        cp.wait()


def solution(mesh):
    n = mesh.shape["seq"]
    ndp = mesh.shape["dp"]
    steps = max(1, n // PLANE - 1)
    gsteps = max(1, (n // PLANE - 1).bit_length() + (ndp - 1).bit_length())

    def local(query_rows, key_rows, value_rows, out_grad, query_gain, key_gain):
        rows, width = query_rows.shape[1:]
        seq_len = rows * n
        score_scale = 1.0 / math.sqrt(HEAD_DIM * seq_len)
        factor = 1.0 / math.sqrt(seq_len * ndp)
        big = jax.ShapeDtypeStruct(query_rows.shape, BF16)
        small = jax.ShapeDtypeStruct((PAIRS, LANES), F32)
        hbm = pl.BlockSpec(memory_space=pltpu.HBM)
        unit = (HEAD_DIM, LANES)
        dma = pltpu.SemaphoreType.DMA
        out = pl.pallas_call(
            functools.partial(kernel, n, ndp, rows, score_scale, factor),
            out_shape=[big, big, big, small, small],
            in_specs=[hbm] * 6,
            out_specs=[pl.BlockSpec(memory_space=pltpu.VMEM)] * 5,
            scratch_shapes=[pltpu.VMEM((rows, width), BF16)] * 6
            + [pltpu.VMEM((PAIRS, LANES), F32)] * 2
            + [pltpu.VMEM((rows, width), F32)] * 3
            + [
                pltpu.VMEM((CHUNKS, 2, PLANE) + unit, F32),
                pltpu.VMEM((CHUNKS, 2, PLANE) + unit, F32),
                pltpu.VMEM((1, CHUNKS, 2) + unit, F32),
                pltpu.VMEM((steps, CHUNKS, 2) + unit, F32),
                pltpu.VMEM((CHUNKS, 2) + unit, F32),
                pltpu.VMEM((CHUNKS, 2, PLANE) + unit, F32),
                pltpu.VMEM((CHUNKS, 2, PLANE) + unit, F32),
                pltpu.VMEM((gsteps + 1, 3, PAIRS, LANES), F32),
                pltpu.VMEM((gsteps, 3, PAIRS, LANES), F32),
                pltpu.VMEM((PLANE, 3, PAIRS, LANES), F32),
                dma((CHUNKS, 4)), dma((2,)),
                dma((CHUNKS, 2, 3)), dma((CHUNKS, 2, 3)),
                dma((steps, CHUNKS, 2)), dma((steps, CHUNKS, 2)),
                dma((CHUNKS, 2, 3)), dma((CHUNKS, 2, 3)),
                dma((gsteps,)), dma((gsteps,)), dma((3,)), dma((3,)),
            ],
            compiler_params=pltpu.CompilerParams(
                collective_id=0, has_side_effects=True, vmem_limit_bytes=32 * 1024 * 1024
            ),
        )(*[pltpu.with_memory_space_constraint(t, pltpu.HBM) for t in (
            query_rows, key_rows, value_rows, out_grad,
            query_gain.reshape(PAIRS, LANES), key_gain.reshape(PAIRS, LANES))])
        out = pl.pallas_call(
            move,
            out_shape=[big, big, big, small, small],
            in_specs=[pl.BlockSpec(memory_space=pltpu.VMEM)] * 5,
            out_specs=[hbm] * 5,
            scratch_shapes=[dma((5,))],
        )(*[pltpu.with_memory_space_constraint(t, pltpu.VMEM) for t in out])
        return (out[0], out[1], out[2], out[3].reshape(width), out[4].reshape(width))

    spec = P("dp", "seq", None)
    return jax.shard_map(local, mesh=mesh, in_specs=(spec,) * 4 + (P(), P()),
                         out_specs=(spec, spec, spec, P(), P()), check_vma=False)
```
